512 devices in a mesh: seq: 64 (over y_lo, z, core), tensor: 8 (over x, y_hi).
Axes of the slice: x: 4, y: 4 (y_hi: 2, y_lo: 2; y = y_hi * 2 + y_lo), z: 16, core: 2. Of those that a mesh axis runs over, the one named last changes fastest.
Arguments:
- trunk: bfloat16 [2, 4096, 1536], P(None, 'seq', 'tensor'), may hold values from -12 to 12
- w_out: bfloat16 [1536, 1536], P('tensor', 'seq'), may hold values from -1 to 1
- gain_coarse: float32 [1536], replicated, may hold values from 0.1 to 1.9
- w_conv1: bfloat16 [5, 1536, 1536], P(None, 'seq', 'tensor'), may hold values from -0.0625 to 0.0625
- w_up: bfloat16 [1536, 2, 768], P('seq', None, 'tensor'), may hold values from -0.15625 to 0.15625
- skip: bfloat16 [2, 8192, 768], P(None, 'seq', 'tensor'), may hold values from -12 to 12
- gain_fine: float32 [768], replicated, may hold values from 0.1 to 1.9
- w_conv2: bfloat16 [5, 768, 768], P(None, 'seq', 'tensor'), may hold values from -0.09375 to 0.09375
- cotangent: bfloat16 [2, 8192, 768], P(None, 'seq', 'tensor'), may hold values from -6 to 6
Outputs:
- decoded: bfloat16 [2, 8192, 768], P(None, 'seq', 'tensor')
- skip_grad: bfloat16 [2, 8192, 768], P(None, 'seq', 'tensor')
- trunk_grad: bfloat16 [2, 4096, 1536], P(None, 'seq', 'tensor')
The draws below stay inside these ranges and needn't reach their ends.
All inputs are finite; a program needn't handle non-finite values.
Results may differ from the reference program's by a relative error of at most 0.02.
Values may be sent and summed in bfloat16 or wider, within the bound.
No kernel may reach another device: no remote copies, remote signals or barrier semaphores. Data moves between devices by JAX's collectives and lax.ppermute only.
A program may use at most 64 MiB of HBM per device.

```python
import math
import jax
import jax.numpy as jnp
from jax import lax

D_TRUNK = 1536
C_COARSE = 1536
C_FINE = 768
SEQS = 2
LENGTH = 4096
N_TENSOR = 8


def log_scales(key, shape):
    return jnp.exp(jax.random.uniform(key, shape, jnp.float32, math.log(0.3), math.log(3.0)))


def draw_trunk(key, part):
    key_a, key_b = jax.random.split(key, 2)
    shape = (SEQS, LENGTH, D_TRUNK)
    rows = log_scales(key_b, (SEQS, LENGTH, 1))
    values = jax.random.normal(key_a, shape, jnp.float32) * rows
    return jnp.clip(values, -12.0, 12.0).astype(jnp.bfloat16)


def draw_w_out(key, part):
    key_a, key_b = jax.random.split(key)
    shape = (D_TRUNK, C_COARSE)
    cols = log_scales(key_b, (1, C_COARSE)) * D_TRUNK ** (-0.5)
    values = jax.random.normal(key_a, shape, jnp.float32) * cols
    return jnp.clip(values, -1.0, 1.0).astype(jnp.bfloat16)


def draw_skip(key, part):
    key_a, key_b = jax.random.split(key, 2)
    shape = (SEQS, 2 * LENGTH, C_FINE)
    cols = log_scales(key_b, (1, 1, C_FINE))
    values = jax.random.normal(key_a, shape, jnp.float32) * cols
    return jnp.clip(values, -12.0, 12.0).astype(jnp.bfloat16)


def block_levels(rng, extent, pieces, least, high):
    loudness, own = 1.0, jax.random.fold_in(rng, 6)
    for position, blocks in pieces:
        heights = jnp.exp(jax.random.uniform(jax.random.fold_in(own, position), (blocks,), jnp.float32, least / len(pieces), high / len(pieces)))
        loudness = loudness * jnp.repeat(heights, extent[position] // blocks).reshape([-1 if axis == position else 1 for axis in range(len(extent))])
    return loudness


def gaussian(rng, extent, spread, bound, cuts=(), held_as=jnp.bfloat16):
    drawn = jax.random.normal(rng, extent, jnp.float32) * spread
    if len(cuts) > 0:
        drawn = block_levels(rng, extent, cuts, -0.22, 0.18) * drawn
    return jnp.clip(drawn, min=-bound, max=bound).astype(held_as)


def setup_inputs(seed: int = 0) -> dict:
    seeds = jax.random.split(jax.random.key(seed), 10)
    trunk = draw_trunk(jax.random.fold_in(seeds[9], 71), 0)
    w_out = draw_w_out(jax.random.fold_in(seeds[9], 71), 0)
    gain_coarse = jnp.clip(1.0 + 0.18 * jax.random.normal(seeds[2], (C_COARSE,), jnp.float32), 0.1, 1.9)
    w_conv1 = gaussian(seeds[3], (5, C_COARSE, C_COARSE), (5 * C_COARSE) ** -0.5, 0.0625, ((1, 64), (2, 8)))
    w_up = gaussian(seeds[4], (C_COARSE, 2, C_FINE), C_COARSE ** -0.5, 0.15625, ((0, 64), (2, 8)))
    skip = draw_skip(jax.random.fold_in(seeds[9], 71), 0)
    gain_fine = jnp.clip(1.0 + 0.18 * jax.random.normal(seeds[6], (C_FINE,), jnp.float32), 0.1, 1.9)
    w_conv2 = gaussian(seeds[7], (5, C_FINE, C_FINE), (5 * C_FINE) ** -0.5, 0.09375, ((1, 64), (2, 8)))
    cotangent = gaussian(seeds[8], (SEQS, 2 * LENGTH, C_FINE), 1.0, 6.0, ((1, 64), (2, 8)))
    return {"trunk": trunk, "w_out": w_out, "gain_coarse": gain_coarse, "w_conv1": w_conv1, "w_up": w_up, "skip": skip, "gain_fine": gain_fine, "w_conv2": w_conv2, "cotangent": cotangent}


EPS = 1e-06

def matmul(left, right):
    flat = jnp.dot(left.reshape(-1, left.shape[-1]), right, preferred_element_type=jnp.float32)
    return flat.reshape(left.shape[:-1] + (right.shape[-1],))

def rounded(value):
    return lax.optimization_barrier(value.astype(jnp.bfloat16)).astype(jnp.float32)

def activate(field, gain):
    scaled = field * lax.rsqrt(lax.optimization_barrier(jnp.mean(field * field, axis=-1, keepdims=True)) + EPS)
    return jax.nn.gelu(scaled * gain)

def conv_ahead(act, weight):
    length = act.shape[1]
    padded = jnp.pad(act, ((0, 0), (2, 2), (0, 0)))
    total = jnp.zeros(act.shape[:2] + (weight.shape[2],), jnp.float32)
    for k in range(5):
        total = total + matmul(padded[:, k:k + length], weight[k])
    return total

def conv_behind(grad, weight):
    length = grad.shape[1]
    padded = jnp.pad(grad, ((0, 0), (2, 2), (0, 0)))
    total = jnp.zeros(grad.shape[:2] + (weight.shape[1],), jnp.float32)
    for k in range(5):
        total = total + matmul(padded[:, 4 - k:4 - k + length], weight[k].T)
    return total

def norm_vjp(field, gain, grad):

    def apply(value):
        return activate(value, gain)
    _, pull = jax.vjp(apply, field.astype(jnp.float32))
    return pull(grad)[0]

def reference(trunk, w_out, gain_coarse, w_conv1, w_up, skip, gain_fine, w_conv2, cotangent):
    groups = N_TENSOR
    hpart = D_TRUNK // groups
    cpart = C_COARSE // groups
    fpart = C_FINE // groups
    seqs = trunk.shape[0]
    length = trunk.shape[1]
    projected = jnp.zeros((seqs, length, C_COARSE), jnp.float32)
    for g in range(groups):
        projected = projected + rounded(matmul(trunk[:, :, g * hpart:(g + 1) * hpart], w_out[g * hpart:(g + 1) * hpart]))
    projected = projected.astype(jnp.bfloat16)
    act_coarse = activate(projected.astype(jnp.float32), gain_coarse).astype(jnp.bfloat16)
    lifted = (projected.astype(jnp.float32) + conv_ahead(act_coarse, w_conv1)).astype(jnp.bfloat16)
    upper = matmul(lifted, w_up.reshape(C_COARSE, 2 * C_FINE)).reshape(seqs, 2 * length, C_FINE)
    merged = (upper + skip.astype(jnp.float32)).astype(jnp.bfloat16)
    act_fine = activate(merged.astype(jnp.float32), gain_fine).astype(jnp.bfloat16)
    decoded = (merged.astype(jnp.float32) + conv_ahead(act_fine, w_conv2)).astype(jnp.bfloat16)
    back_fine = jnp.zeros((seqs, 2 * length, C_FINE), jnp.float32)
    for g in range(groups):
        back_fine = back_fine + rounded(conv_behind(cotangent[:, :, g * fpart:(g + 1) * fpart], w_conv2[:, :, g * fpart:(g + 1) * fpart]))
    skip_grad = (cotangent.astype(jnp.float32) + norm_vjp(merged, gain_fine, back_fine)).astype(jnp.bfloat16)
    lifted_grad = jnp.zeros((seqs, length, C_COARSE), jnp.float32)
    for g in range(groups):
        piece = skip_grad[:, :, g * fpart:(g + 1) * fpart].reshape(seqs, length, 2 * fpart)
        wpiece = w_up[:, :, g * fpart:(g + 1) * fpart].reshape(C_COARSE, 2 * fpart)
        lifted_grad = lifted_grad + rounded(matmul(piece, wpiece.T))
    lifted_grad = lifted_grad.astype(jnp.bfloat16)
    back_coarse = jnp.zeros((seqs, length, C_COARSE), jnp.float32)
    for g in range(groups):
        back_coarse = back_coarse + rounded(conv_behind(lifted_grad[:, :, g * cpart:(g + 1) * cpart], w_conv1[:, :, g * cpart:(g + 1) * cpart]))
    projected_grad = (lifted_grad.astype(jnp.float32) + norm_vjp(projected, gain_coarse, back_coarse)).astype(jnp.bfloat16)
    trunk_grad = matmul(projected_grad, w_out.T).astype(jnp.bfloat16)
    return (decoded, skip_grad, trunk_grad)
```

```python
import jax
import jax.numpy as jnp
from jax import lax
from jax.sharding import PartitionSpec as P

C_COARSE = 1536
C_FINE = 768
EPS = 1e-06
BF16 = jnp.bfloat16
F32 = jnp.float32
NT = 8
ZS = 16
Y_PAIRS = [[y * 32 + i for y in range(2)] for i in range(32)]
Z_CORES = [[y * 32 + i for i in range(32)] for y in range(2)]


def dot(left, right):
    return lax.dot_general(
        left, right, (((left.ndim - 1,), (0,)), ((), ())), preferred_element_type=F32
    )


def dot_t(left, right):
    return lax.dot_general(
        left,
        right,
        (((left.ndim - 1,), (right.ndim - 1,)), ((), ())),
        preferred_element_type=F32,
    )


def exchange(blocks):
    return lax.all_to_all(blocks, "tensor", 0, 0)


def share(piece):
    return exchange(jnp.broadcast_to(piece[None], (NT,) + piece.shape))


def neighbours(shard, width):
    size, length = lax.axis_size("seq"), shard.shape[1]
    up = [(i, i + 1) for i in range(size - 1)]
    down = [(j, i) for i, j in up]
    before = lax.ppermute(shard[:, length - width :], "seq", up)
    after = lax.ppermute(shard[:, :width], "seq", down)
    return jnp.concatenate([before, shard, after], axis=1)


def lanes(blocks):
    moved = jnp.moveaxis(blocks, 0, 2)
    return moved.reshape(moved.shape[:2] + (-1,))


def split(full):
    return jnp.moveaxis(full.reshape(full.shape[:2] + (NT, -1)), 2, 0)


def per_device(trunk, w_out, gain_coarse, w_conv1, w_up, skip, gain_fine, w_conv2, cotangent):
    rank = lax.axis_index("tensor")
    place = lax.axis_index("seq")
    part_coarse, part_fine = C_COARSE // NT, C_FINE // NT
    seqs, slab = trunk.shape[0], trunk.shape[1]

    turned = [
        ((8 * a + b) * NT + t, (8 * t + b) * NT + a)
        for a in range(8)
        for b in range(8)
        for t in range(8)
    ]
    up_shard = w_up.reshape(24, 192)
    up_turned = lax.ppermute(up_shard, ("seq", "tensor"), turned)
    conv1_shard = jnp.transpose(w_conv1, (1, 0, 2)).reshape(24, 960)
    conv2_flat = jnp.transpose(w_conv2, (1, 0, 2)).reshape(12, 480)
    conv2_shard = jnp.concatenate([conv2_flat[:, :240], conv2_flat[:, 240:]], axis=0)
    packed = jnp.concatenate(
        [w_out.T, conv1_shard, up_shard, up_turned, conv2_shard, jnp.zeros((24, 80), BF16)],
        axis=1,
    )
    paired = lax.all_gather(packed, "seq", axis=0, axis_index_groups=Y_PAIRS)
    gathered = lax.all_gather(
        paired[:, :, 192:], "seq", axis=1, tiled=True, axis_index_groups=Z_CORES
    )
    out_t = lax.all_gather(
        paired[:, :, :192], "seq", axis=1, tiled=True, axis_index_groups=Z_CORES
    ).reshape(C_COARSE, part_coarse)
    flat = gathered.reshape(C_COARSE, -1)
    conv1_w = flat[:, :960]
    up_w = flat[:, 960:1152]
    up_turned_w = flat[:, 1152:1344].reshape(NT, part_coarse, 192)
    conv2_w = (
        gathered[:, :, 1344:1584]
        .reshape(2, 32, 2, 12, 240)
        .transpose(0, 1, 3, 2, 4)
        .reshape(C_FINE, 480)
    )

    trunk_ext = neighbours(trunk, 4)
    skip_ext = neighbours(skip, 4)
    cot_ext = neighbours(cotangent, 6)
    fine_rows = 2 * slab + 8
    index = place * 2 * slab - 4 + lax.broadcasted_iota(jnp.int32, (1, fine_rows, 1), 1)
    inside = (index >= 0) & (index < 2 * slab * lax.axis_size("seq"))

    partial = dot_t(trunk_ext, out_t).astype(BF16)
    projected = jnp.sum(exchange(split(partial)).astype(F32), axis=0).astype(BF16)
    projected_full = lanes(share(projected)).astype(F32)
    scale_coarse = lax.rsqrt(
        jnp.mean(projected_full * projected_full, axis=-1, keepdims=True) + EPS
    )
    act_coarse = jax.nn.gelu(projected_full * scale_coarse * gain_coarse).astype(BF16)
    cot_full = lanes(share(cot_ext[:, 2 : 2 + fine_rows]))

    taps = dot(act_coarse, conv1_w)
    rows = slab + 4
    mixed = sum(
        taps[:, k : k + rows, k * part_coarse : (k + 1) * part_coarse] for k in range(5)
    )
    lifted = (projected[:, 2 : 2 + rows].astype(F32) + mixed).astype(BF16)

    stacked = jnp.concatenate([cot_ext[:, 4 - k : 4 - k + fine_rows] for k in range(5)], axis=2)
    back_partial = split(dot_t(stacked, conv2_w).astype(BF16))
    first = exchange(
        jnp.concatenate(
            [
                jnp.broadcast_to(lifted[None], (NT,) + lifted.shape),
                back_partial.reshape(NT, seqs, rows, 2 * part_fine),
            ],
            axis=1,
        )
    )
    lifted_full = lanes(first[:, :seqs])
    back_piece = jnp.sum(first[:, seqs:].astype(F32), axis=0).astype(BF16)
    upper = dot(lifted_full, up_w).reshape(seqs, fine_rows, part_fine)
    merged = jnp.where(inside, upper + skip_ext.astype(F32), 0.0).astype(BF16)
    second = share(
        jnp.concatenate([merged, back_piece.reshape(seqs, fine_rows, part_fine)], axis=0)
    )
    merged_full = lanes(second[:, :seqs]).astype(F32)
    back_fine = lanes(second[:, seqs:]).astype(F32)

    def activate(value):
        scaled = value * lax.rsqrt(jnp.mean(value * value, axis=-1, keepdims=True) + EPS)
        return jax.nn.gelu(scaled * gain_fine)

    act_fine, pull = jax.vjp(activate, merged_full)
    skip_grad_full = jnp.where(
        inside, cot_full.astype(F32) + pull(back_fine)[0], 0.0
    ).astype(BF16)
    folded = skip_grad_full.reshape(seqs, rows, 2, NT, part_fine)
    lifted_grad = sum(
        dot_t(folded[:, :, :, t].reshape(seqs, rows, 2 * part_fine), up_turned_w[t])
        for t in range(NT)
    ).astype(BF16)
    stacked_grad = jnp.concatenate(
        [lifted_grad[:, 4 - k : 4 - k + slab] for k in range(5)], axis=2
    )
    third = exchange(split(dot_t(stacked_grad, conv1_w).astype(BF16)))
    back_coarse = jnp.sum(third.astype(F32), axis=0)

    own = projected[:, 4 : 4 + slab].astype(F32)
    own_gain = lax.dynamic_slice_in_dim(gain_coarse, rank * part_coarse, part_coarse, 0)
    scale = scale_coarse[:, 4 : 4 + slab]
    _, pull_gelu = jax.vjp(jax.nn.gelu, own * scale * own_gain)
    inner = pull_gelu(back_coarse)[0] * own_gain
    share_sum = jnp.sum(inner * own, axis=-1, keepdims=True)
    high = share_sum.astype(BF16)
    low = (share_sum - high.astype(F32)).astype(BF16)
    direct = (lifted_grad[:, 2 : 2 + slab].astype(F32) + scale * inner).astype(BF16)
    fourth = share(
        jnp.concatenate([direct, high, low, jnp.zeros((seqs, slab, 62), BF16)], axis=2)
    )
    total = jnp.sum(fourth[..., 192:194].astype(F32), axis=(0, 3))[..., None]
    factor = scale * scale * scale * total * (1.0 / C_COARSE)
    projected_grad = (
        lanes(fourth[..., :192]).astype(F32) - projected_full[:, 4 : 4 + slab] * factor
    ).astype(BF16)
    trunk_grad = dot(projected_grad, out_t).astype(BF16)

    fine_taps = dot(act_fine.astype(BF16), conv2_w)
    fine_mixed = sum(
        fine_taps[:, 2 + k : 2 + k + 2 * slab, k * part_fine : (k + 1) * part_fine]
        for k in range(5)
    )
    keep = slice(4, 4 + 2 * slab)
    decoded = (merged[:, keep].astype(F32) + fine_mixed).astype(BF16)
    skip_grad = lax.dynamic_slice_in_dim(
        skip_grad_full[:, keep], rank * part_fine, part_fine, 2
    )
    return (decoded, skip_grad, trunk_grad)


def solution(mesh):
    in_specs = (
        P(None, "seq", "tensor"),
        P("tensor", "seq"),
        P(),
        P(None, "seq", "tensor"),
        P("seq", None, "tensor"),
        P(None, "seq", "tensor"),
        P(),
        P(None, "seq", "tensor"),
        P(None, "seq", "tensor"),
    )
    out_specs = (P(None, "seq", "tensor"), P(None, "seq", "tensor"), P(None, "seq", "tensor"))
    return jax.shard_map(
        per_device, mesh=mesh, in_specs=in_specs, out_specs=out_specs, check_vma=False
    )
```

```python
import jax
import jax.numpy as jnp
from jax import lax
from jax.experimental.layout import Layout, with_layout_constraint
from jax.sharding import PartitionSpec as P

C_COARSE = 1536
C_FINE = 768
EPS = 1e-06
BF16 = jnp.bfloat16
F32 = jnp.float32
NT = 8
Y_PAIRS = [[y * 32 + i for y in range(2)] for i in range(32)]
Z_CORES = [[y * 32 + i for i in range(32)] for y in range(2)]


def dot(left, right):
    return lax.dot_general(
        left, right, (((left.ndim - 1,), (0,)), ((), ())), preferred_element_type=F32
    )


def dot_t(left, right):
    return lax.dot_general(
        left,
        right,
        (((left.ndim - 1,), (right.ndim - 1,)), ((), ())),
        preferred_element_type=F32,
    )


def exchange(blocks):
    return lax.all_to_all(blocks, "tensor", 0, 0)


def share(piece):
    return exchange(jnp.broadcast_to(piece[None], (NT,) + piece.shape))


def neighbours(shard, width):
    size, length = lax.axis_size("seq"), shard.shape[1]
    up = [(i, i + 1) for i in range(size - 1)]
    down = [(j, i) for i, j in up]
    before = lax.ppermute(shard[:, length - width :], "seq", up)
    after = lax.ppermute(shard[:, :width], "seq", down)
    return jnp.concatenate([before, shard, after], axis=1)


def lanes(blocks):
    moved = jnp.moveaxis(blocks, 0, 2)
    return moved.reshape(moved.shape[:2] + (-1,))


def split(full):
    return jnp.moveaxis(full.reshape(full.shape[:2] + (NT, -1)), 2, 0)


def per_device(trunk, w_out, gain_coarse, w_conv1, w_up, skip, gain_fine, w_conv2, cotangent):
    rank = lax.axis_index("tensor")
    place = lax.axis_index("seq")
    part_coarse, part_fine = C_COARSE // NT, C_FINE // NT
    seqs, slab = trunk.shape[0], trunk.shape[1]

    turned = [
        ((8 * a + b) * NT + t, (8 * t + b) * NT + a)
        for a in range(8)
        for b in range(8)
        for t in range(8)
    ]
    up_shard = w_up.reshape(24, 192)
    out_shard = w_out.T
    both_turned = lax.ppermute(
        jnp.concatenate([out_shard, up_shard], axis=1), ("seq", "tensor"), turned
    )
    conv1_shard = jnp.transpose(w_conv1, (1, 0, 2)).reshape(24, 960)
    conv2_flat = jnp.transpose(w_conv2, (1, 0, 2)).reshape(12, 480)
    conv2_shard = jnp.concatenate([conv2_flat[:, :240], conv2_flat[:, 240:]], axis=0)
    packed = jnp.concatenate(
        [
            both_turned[:, :192],
            conv1_shard,
            up_shard,
            both_turned[:, 192:],
            out_shard,
            conv2_shard,
            jnp.zeros((24, 16), BF16),
        ],
        axis=1,
    )
    paired = lax.all_gather(packed, "seq", axis=0, axis_index_groups=Y_PAIRS)
    gathered = lax.all_gather(
        paired[:, :, 192:], "seq", axis=1, tiled=True, axis_index_groups=Z_CORES
    )
    gathered = with_layout_constraint(gathered, Layout(major_to_minor=(0, 1, 2)))
    flat = gathered.reshape(C_COARSE, -1)
    conv1_w = flat[:, :960]
    up_w = flat[:, 960:1152]
    up_turned_w = flat[:, 1152:1344].reshape(NT, part_coarse, 192)
    out_t = flat[:, 1344:1536]
    conv2_w = (
        gathered[:, :, 1536:1776]
        .reshape(2, 32, 2, 12, 240)
        .transpose(0, 1, 3, 2, 4)
        .reshape(C_FINE, 480)
    )

    trunk_ext = neighbours(trunk, 4)
    skip_ext = neighbours(skip, 4)
    cot_ext = neighbours(cotangent, 8)
    fine_rows = 2 * slab + 8
    index = place * 2 * slab - 4 + lax.broadcasted_iota(jnp.int32, (1, fine_rows, 1), 1)
    inside = (index >= 0) & (index < 2 * slab * lax.axis_size("seq"))

    both = share(
        jnp.concatenate([trunk_ext, cot_ext.reshape(seqs, slab + 8, 2 * part_fine)], axis=0)
    )
    trunk_blocks = both[:, :seqs]
    cot_blocks = both[:, seqs:].reshape(NT, seqs, 2 * slab + 16, part_fine)
    cot_blocks = cot_blocks[:, :, 4 : 4 + fine_rows]
    out_turned = lax.all_gather(
        paired[:, :, :192], "seq", axis=1, tiled=True, axis_index_groups=Z_CORES
    ).reshape(NT, part_coarse, 192)
    projected = lax.dot_general(
        trunk_blocks, out_turned, (((0, 3), (0, 2)), ((), ())), preferred_element_type=F32
    ).astype(BF16)
    projected_full = lanes(share(projected)).astype(F32)
    scale_coarse = lax.rsqrt(
        jnp.mean(projected_full * projected_full, axis=-1, keepdims=True) + EPS
    )
    act_coarse = jax.nn.gelu(projected_full * scale_coarse * gain_coarse).astype(BF16)
    cot_full = lanes(cot_blocks)

    taps = dot(act_coarse, conv1_w)
    rows = slab + 4
    mixed = sum(
        taps[:, k : k + rows, k * part_coarse : (k + 1) * part_coarse] for k in range(5)
    )
    lifted = (projected[:, 2 : 2 + rows].astype(F32) + mixed).astype(BF16)

    stacked = jnp.concatenate([cot_ext[:, 6 - k : 6 - k + fine_rows] for k in range(5)], axis=2)
    back_partial = split(dot_t(stacked, conv2_w).astype(BF16))
    first = exchange(
        jnp.concatenate(
            [
                jnp.broadcast_to(lifted[None], (NT,) + lifted.shape),
                back_partial.reshape(NT, seqs, rows, 2 * part_fine),
            ],
            axis=1,
        )
    )
    lifted_full = lanes(first[:, :seqs])
    back_piece = jnp.sum(first[:, seqs:].astype(F32), axis=0).astype(BF16)
    upper = dot(lifted_full, up_w).reshape(seqs, fine_rows, part_fine)
    merged = jnp.where(inside, upper + skip_ext.astype(F32), 0.0).astype(BF16)
    second = share(
        jnp.concatenate([merged, back_piece.reshape(seqs, fine_rows, part_fine)], axis=0)
    )
    merged_full = lanes(second[:, :seqs]).astype(F32)
    back_fine = lanes(second[:, seqs:]).astype(F32)

    def activate(value):
        scaled = value * lax.rsqrt(jnp.mean(value * value, axis=-1, keepdims=True) + EPS)
        return jax.nn.gelu(scaled * gain_fine)

    act_fine, pull = jax.vjp(activate, merged_full)
    skip_grad_full = jnp.where(
        inside, cot_full.astype(F32) + pull(back_fine)[0], 0.0
    ).astype(BF16)
    folded = skip_grad_full.reshape(seqs, rows, 2, NT, part_fine)
    lifted_grad = lax.dot_general(
        folded, up_turned_w.reshape(NT, part_coarse, 2, part_fine),
        (((2, 3, 4), (2, 0, 3)), ((), ())),
        preferred_element_type=F32,
    ).astype(BF16)
    stacked_grad = jnp.concatenate(
        [lifted_grad[:, 4 - k : 4 - k + slab] for k in range(5)], axis=2
    )
    third = exchange(split(dot_t(stacked_grad, conv1_w).astype(BF16)))
    back_coarse = jnp.sum(third.astype(F32), axis=0)

    own = projected[:, 4 : 4 + slab].astype(F32)
    own_gain = lax.dynamic_slice_in_dim(gain_coarse, rank * part_coarse, part_coarse, 0)
    scale = scale_coarse[:, 4 : 4 + slab]
    _, pull_gelu = jax.vjp(jax.nn.gelu, own * scale * own_gain)
    inner = pull_gelu(back_coarse)[0] * own_gain
    share_sum = jnp.sum(inner * own, axis=-1, keepdims=True)
    high = share_sum.astype(BF16)
    low = (share_sum - high.astype(F32)).astype(BF16)
    direct = (lifted_grad[:, 2 : 2 + slab].astype(F32) + scale * inner).astype(BF16)
    fourth = share(
        jnp.concatenate([direct, high, low, jnp.zeros((seqs, slab, 62), BF16)], axis=2)
    )
    total = jnp.sum(fourth[..., 192:194].astype(F32), axis=(0, 3))[..., None]
    factor = scale * scale * scale * total * (1.0 / C_COARSE)
    projected_grad = (
        lanes(fourth[..., :192]).astype(F32) - projected_full[:, 4 : 4 + slab] * factor
    ).astype(BF16)
    trunk_grad = dot(projected_grad, out_t).astype(BF16)

    fine_taps = dot(act_fine.astype(BF16), conv2_w)
    fine_mixed = sum(
        fine_taps[:, 2 + k : 2 + k + 2 * slab, k * part_fine : (k + 1) * part_fine]
        for k in range(5)
    )
    keep = slice(4, 4 + 2 * slab)
    decoded = (merged[:, keep].astype(F32) + fine_mixed).astype(BF16)
    skip_grad = lax.dynamic_slice_in_dim(
        skip_grad_full[:, keep], rank * part_fine, part_fine, 2
    )
    return (decoded, skip_grad, trunk_grad)


def solution(mesh):
    in_specs = (
        P(None, "seq", "tensor"),
        P("tensor", "seq"),
        P(),
        P(None, "seq", "tensor"),
        P("seq", None, "tensor"),
        P(None, "seq", "tensor"),
        P(),
        P(None, "seq", "tensor"),
        P(None, "seq", "tensor"),
    )
    out_specs = (P(None, "seq", "tensor"), P(None, "seq", "tensor"), P(None, "seq", "tensor"))

    return jax.shard_map(
        per_device, mesh=mesh, in_specs=in_specs, out_specs=out_specs, check_vma=False
    )
```

```python
import math

import jax
import jax.numpy as jnp
from jax import lax
from jax.experimental import pallas as pl
from jax.experimental.layout import Layout, with_layout_constraint
from jax.experimental.pallas import tpu as pltpu
from jax.sharding import PartitionSpec as P

C_COARSE = 1536
C_FINE = 768
EPS = 1e-06
SQRT_2_PI = math.sqrt(2.0 / math.pi)
BF16 = jnp.bfloat16
F32 = jnp.float32
NT = 8
Y_PAIRS = [[y * 32 + i for y in range(2)] for i in range(32)]
Z_CORES = [[y * 32 + i for i in range(32)] for y in range(2)]


def dot(left, right):
    return lax.dot_general(
        left, right, (((left.ndim - 1,), (0,)), ((), ())), preferred_element_type=F32
    )


def dot_t(left, right):
    return lax.dot_general(
        left,
        right,
        (((left.ndim - 1,), (right.ndim - 1,)), ((), ())),
        preferred_element_type=F32,
    )


def exchange(blocks):
    return lax.all_to_all(blocks, "tensor", 0, 0)


def share(piece):
    return exchange(jnp.broadcast_to(piece[None], (NT,) + piece.shape))


def neighbours(shard, width):
    size, length = lax.axis_size("seq"), shard.shape[1]
    up = [(i, i + 1) for i in range(size - 1)]
    down = [(j, i) for i, j in up]
    before = lax.ppermute(shard[:, length - width :], "seq", up)
    after = lax.ppermute(shard[:, :width], "seq", down)
    return jnp.concatenate([before, shard, after], axis=1)


def lanes(blocks):
    moved = jnp.moveaxis(blocks, 0, 2)
    return moved.reshape(moved.shape[:2] + (-1,))


def split(full):
    return jnp.moveaxis(full.reshape(full.shape[:2] + (NT, -1)), 2, 0)


def fine_adjoint(shared_ref, cot_ref, gain_ref, inside_ref, up_ref, conv_ref, back_ref, grad_ref, lifted_ref, norm_ref, rows_ref, taps_ref):
    slab, rows = back_ref.shape[2], rows_ref.shape[1]
    for p in range(2):
        square = jnp.zeros(shared_ref.shape[2:], F32)
        for t in range(NT):
            value = shared_ref[t, p].astype(F32)
            square = square + value * value
        mean = jnp.sum(square, axis=-1, keepdims=True) * (1.0 / C_FINE)
        scale = lax.rsqrt(mean + EPS)
        weighted = jnp.zeros(shared_ref.shape[2:], F32)
        for t in range(NT):
            value = shared_ref[t, p].astype(F32)
            gain = gain_ref[t]
            inner = slope(value * scale * gain) * shared_ref[t, 2 + p].astype(F32) * gain
            weighted = weighted + inner * value
            norm_ref[t] = inner * scale
        total = jnp.sum(weighted, axis=-1, keepdims=True)
        factor = scale * scale * scale * total * (1.0 / C_FINE)
        keep = inside_ref[p] > 0.0
        lifted = jnp.zeros((shared_ref.shape[2], up_ref.shape[2]), F32)
        for t in range(NT):
            value = shared_ref[t, p].astype(F32)
            grad = cot_ref[t, p].astype(F32) + (norm_ref[t] - value * factor)
            grad = jnp.where(keep, grad, 0.0).astype(BF16)
            grad_ref[t, p] = grad
            lifted = lifted + dot_t(grad, up_ref[p, t])
        if p == 0:
            first = lifted
        else:
            lifted = (first + lifted).astype(BF16).astype(F32)
    for s in range(2):
        rows_ref[s] = lifted[s * rows : (s + 1) * rows]
        lifted_ref[s] = rows_ref[s, 2 : 2 + slab, :192].astype(BF16)
        for k in range(5):
            taps_ref[s * slab : (s + 1) * slab, k * 128 : (k + 1) * 128] = rows_ref[
                s, 4 - k : 4 - k + slab, :128
            ].astype(BF16)
        for k in (0, 2, 4):
            tail = rows_ref[s, 4 - k : 4 - k + slab, 128:256]
            if k < 4:
                tail = tail + pltpu.roll(rows_ref[s, 3 - k : 3 - k + slab, 128:256], 64, 1)
            taps_ref[s * slab : (s + 1) * slab, 640 + k * 64 : 768 + k * 64] = tail.astype(BF16)
    for t in range(NT):
        back = dot_t(taps_ref[...], conv_ref[192 * t : 192 * (t + 1), :]).astype(BF16)
        for s in range(2):
            back_ref[t, s] = back[s * slab : (s + 1) * slab]


def slope(value):
    square = value * value
    bend = jnp.tanh(SQRT_2_PI * (value + 0.044715 * (square * value)))
    half = 0.5 * (1.0 + bend)
    return half + 0.5 * value * (1.0 - bend * bend) * (
        SQRT_2_PI * (1.0 + (3 * 0.044715) * square)
    )


def run_fine_adjoint(shared, cot, gain, inside, up_phases, flat, slab):
    whole = pl.BlockSpec(memory_space=pltpu.VMEM)
    rows = shared.shape[2] // 2
    return pl.pallas_call(
        fine_adjoint,
        grid=(1,),
        in_specs=[whole] * 5 + [pl.BlockSpec((C_COARSE, 1024), lambda i: (0, 0))],
        out_specs=[whole] * 3,
        out_shape=[
            jax.ShapeDtypeStruct((NT, 2, slab, 192), BF16),
            jax.ShapeDtypeStruct(cot.shape, BF16),
            jax.ShapeDtypeStruct((2, slab, 192), BF16),
        ],
        scratch_shapes=[
            pltpu.VMEM((NT,) + shared.shape[2:], F32),
            pltpu.VMEM((2, rows, 256), F32),
            pltpu.VMEM((2 * slab, 1024), BF16),
        ],
        compiler_params=pltpu.CompilerParams(vmem_limit_bytes=40 * 2**20),
        name="fine_adjoint",
    )(shared, cot, gain, inside, up_phases, flat)


def per_device(trunk, w_out, gain_coarse, w_conv1, w_up, skip, gain_fine, w_conv2, cotangent):
    rank = lax.axis_index("tensor")
    place = lax.axis_index("seq")
    part_coarse, part_fine = C_COARSE // NT, C_FINE // NT
    seqs, slab = trunk.shape[0], trunk.shape[1]

    turned = [
        ((8 * a + b) * NT + t, (8 * t + b) * NT + a)
        for a in range(8)
        for b in range(8)
        for t in range(8)
    ]
    up_shard = w_up.reshape(24, 192)
    out_shard = w_out.T
    both_turned = lax.ppermute(
        jnp.concatenate([out_shard, up_shard], axis=1), ("seq", "tensor"), turned
    )
    conv1_turned = jnp.transpose(w_conv1, (1, 0, 2))
    conv1_shard = jnp.concatenate(
        [conv1_turned[:, :, :128].reshape(24, 640), conv1_turned[:, :, 128:].reshape(24, 320)],
        axis=1,
    )
    conv2_flat = jnp.transpose(w_conv2, (1, 0, 2)).reshape(12, 480)
    conv2_shard = jnp.concatenate([conv2_flat[:, :240], conv2_flat[:, 240:]], axis=0)
    packed = jnp.concatenate(
        [
            both_turned[:, :192],
            conv1_shard,
            jnp.zeros((24, 64), BF16),
            up_shard,
            both_turned[:, 192:],
            out_shard,
            conv2_shard,
            jnp.zeros((24, 80), BF16),
        ],
        axis=1,
    )
    paired = lax.all_gather(packed, "seq", axis=0, axis_index_groups=Y_PAIRS)
    gathered = lax.all_gather(
        paired[:, :, 192:], "seq", axis=1, tiled=True, axis_index_groups=Z_CORES
    )
    gathered = with_layout_constraint(gathered, Layout(major_to_minor=(0, 1, 2)))
    flat = gathered.reshape(C_COARSE, -1)
    conv1_w = flat[:, :960]
    up_w = flat[:, 1024:1216]
    up_turned_w = flat[:, 1216:1408].reshape(NT, part_coarse, 192)
    out_t = flat[:, 1408:1600]
    conv2_w = (
        gathered[:, :, 1600:1840]
        .reshape(2, 32, 2, 12, 240)
        .transpose(0, 1, 3, 2, 4)
        .reshape(C_FINE, 480)
    )

    trunk_ext = neighbours(trunk, 4)
    skip_ext = neighbours(skip, 4)
    cot_ext = neighbours(cotangent, 8)
    fine_rows = 2 * slab + 8
    index = place * slab - 2 + lax.broadcasted_iota(jnp.int32, (1, slab + 4, 1), 1)
    inside = (index >= 0) & (index < slab * lax.axis_size("seq"))
    inside_rows = jnp.broadcast_to(inside, (2, 2, slab + 4, 1)).astype(F32)
    skip_phases = jnp.moveaxis(skip_ext.reshape(seqs, slab + 4, 2, part_fine), 2, 0)

    both = share(
        jnp.concatenate([trunk_ext, cot_ext.reshape(seqs, slab + 8, 2 * part_fine)], axis=0)
    )
    trunk_blocks = both[:, :seqs]
    cot_blocks = both[:, seqs:].reshape(NT, seqs, 2 * slab + 16, part_fine)
    cot_blocks = cot_blocks[:, :, 4 : 4 + fine_rows]
    out_turned = lax.all_gather(
        paired[:, :, :192], "seq", axis=1, tiled=True, axis_index_groups=Z_CORES
    ).reshape(NT, part_coarse, 192)
    projected = lax.dot_general(
        trunk_blocks, out_turned, (((0, 3), (0, 2)), ((), ())), preferred_element_type=F32
    ).astype(BF16)
    projected_full = lanes(share(projected)).astype(F32)
    scale_coarse = lax.rsqrt(
        jnp.mean(projected_full * projected_full, axis=-1, keepdims=True) + EPS
    )
    act_coarse = jax.nn.gelu(projected_full * scale_coarse * gain_coarse).astype(BF16)

    taps = dot(act_coarse, conv1_w)
    rows = slab + 4
    wide = sum(taps[:, k : k + rows, k * 128 : (k + 1) * 128] for k in range(5))
    tail = sum(taps[:, k : k + rows, 640 + k * 64 : 704 + k * 64] for k in range(5))
    mixed = jnp.concatenate([wide, tail], axis=2)
    lifted = (projected[:, 2 : 2 + rows].astype(F32) + mixed).astype(BF16)

    stacked = jnp.concatenate([cot_ext[:, 6 - k : 6 - k + fine_rows] for k in range(5)], axis=2)
    back_partial = split(dot_t(stacked, conv2_w).astype(BF16))
    first = exchange(
        jnp.concatenate(
            [
                jnp.broadcast_to(lifted[None], (NT,) + lifted.shape),
                back_partial.reshape(NT, seqs, rows, 2 * part_fine),
            ],
            axis=1,
        )
    )
    lifted_full = lanes(first[:, :seqs])
    back_piece = jnp.sum(first[:, seqs:].astype(F32), axis=0).astype(BF16)
    upper = dot(lifted_full, up_w)
    upper = jnp.stack([upper[..., :part_fine], upper[..., part_fine:]])
    merged = jnp.where(inside, upper + skip_phases.astype(F32), 0.0).astype(BF16)
    back_piece = jnp.stack([back_piece[..., :part_fine], back_piece[..., part_fine:]])
    second = share(
        jnp.concatenate([merged, back_piece], axis=0).reshape(4, seqs * rows, part_fine)
    )

    cot_phases = (
        cot_blocks.reshape(NT, seqs, rows, 2, part_fine)
        .transpose(0, 3, 1, 2, 4)
        .reshape(NT, 2, seqs * rows, part_fine)
    )
    up_phases = jnp.pad(
        up_turned_w.reshape(NT, part_coarse, 2, part_fine).transpose(2, 0, 1, 3),
        ((0, 0), (0, 0), (0, 64), (0, 0)),
    )
    back_blocks, grad_blocks, lifted_grad = run_fine_adjoint(
        second,
        cot_phases,
        gain_fine.reshape(NT, 1, part_fine),
        inside_rows.reshape(2, seqs * rows, 1),
        up_phases,
        flat,
        slab,
    )
    third = exchange(back_blocks)
    back_coarse = jnp.sum(third.astype(F32), axis=0)

    own = projected[:, 4 : 4 + slab].astype(F32)
    own_gain = lax.dynamic_slice_in_dim(gain_coarse, rank * part_coarse, part_coarse, 0)
    scale = scale_coarse[:, 4 : 4 + slab]
    _, pull_gelu = jax.vjp(jax.nn.gelu, own * scale * own_gain)
    inner = pull_gelu(back_coarse)[0] * own_gain
    share_sum = jnp.sum(inner * own, axis=-1, keepdims=True)
    high = share_sum.astype(BF16)
    low = (share_sum - high.astype(F32)).astype(BF16)
    direct = (lifted_grad.astype(F32) + scale * inner).astype(BF16)
    fourth = share(
        jnp.concatenate([direct, high, low, jnp.zeros((seqs, slab, 62), BF16)], axis=2)
    )
    total = jnp.sum(fourth[..., 192:194].astype(F32), axis=(0, 3))[..., None]
    factor = scale * scale * scale * total * (1.0 / C_COARSE)
    projected_grad = (
        lanes(fourth[..., :192]).astype(F32) - projected_full[:, 4 : 4 + slab] * factor
    ).astype(BF16)
    trunk_grad = dot(projected_grad, out_t).astype(BF16)

    merged_full = (
        second[:, :2]
        .reshape(NT, 2, seqs, rows, part_fine)
        .transpose(2, 3, 1, 0, 4)
        .reshape(seqs, fine_rows, C_FINE)
        .astype(F32)
    )
    scaled = merged_full * lax.rsqrt(
        jnp.mean(merged_full * merged_full, axis=-1, keepdims=True) + EPS
    )
    act_fine = jax.nn.gelu(scaled * gain_fine).astype(BF16)
    fine_taps = dot(act_fine, conv2_w)
    fine_mixed = sum(
        fine_taps[:, 2 + k : 2 + k + 2 * slab, k * part_fine : (k + 1) * part_fine]
        for k in range(5)
    )

    def natural(phases):
        moved = jnp.moveaxis(phases.reshape(2, seqs, rows, part_fine)[:, :, 2 : 2 + slab], 0, 2)
        return moved.reshape(seqs, 2 * slab, part_fine)

    decoded = (natural(merged).astype(F32) + fine_mixed).astype(BF16)
    skip_grad = natural(lax.dynamic_index_in_dim(grad_blocks, rank, 0, keepdims=False))
    return (decoded, skip_grad, trunk_grad)


def solution(mesh):
    in_specs = (
        P(None, "seq", "tensor"),
        P("tensor", "seq"),
        P(),
        P(None, "seq", "tensor"),
        P("seq", None, "tensor"),
        P(None, "seq", "tensor"),
        P(),
        P(None, "seq", "tensor"),
        P(None, "seq", "tensor"),
    )
    out_specs = (P(None, "seq", "tensor"), P(None, "seq", "tensor"), P(None, "seq", "tensor"))

    return jax.shard_map(
        per_device, mesh=mesh, in_specs=in_specs, out_specs=out_specs, check_vma=False
    )
```

```python
import math

import jax
import jax.numpy as jnp
from jax import lax
from jax.experimental import pallas as pl
from jax.experimental.layout import Layout, with_layout_constraint
from jax.experimental.pallas import tpu as pltpu
from jax.sharding import PartitionSpec as P

C_COARSE = 1536
C_FINE = 768
EPS = 1e-06
SQRT_2_PI = math.sqrt(2.0 / math.pi)
BF16 = jnp.bfloat16
F32 = jnp.float32
NT = 8
Y_PAIRS = [[y * 32 + i for y in range(2)] for i in range(32)]
Z_CORES = [[y * 32 + i for i in range(32)] for y in range(2)]


def dot(left, right):
    return lax.dot_general(
        left, right, (((left.ndim - 1,), (0,)), ((), ())), preferred_element_type=F32
    )


def dot_t(left, right):
    return lax.dot_general(
        left,
        right,
        (((left.ndim - 1,), (right.ndim - 1,)), ((), ())),
        preferred_element_type=F32,
    )


def exchange(blocks):
    return lax.all_to_all(blocks, "tensor", 0, 0)


def share(piece):
    return exchange(jnp.broadcast_to(piece[None], (NT,) + piece.shape))


def neighbours(shard, width):
    size, length = lax.axis_size("seq"), shard.shape[1]
    up = [(i, i + 1) for i in range(size - 1)]
    down = [(j, i) for i, j in up]
    before = lax.ppermute(shard[:, length - width :], "seq", up)
    after = lax.ppermute(shard[:, :width], "seq", down)
    return jnp.concatenate([before, shard, after], axis=1)


def lanes(blocks):
    moved = jnp.moveaxis(blocks, 0, 2)
    return moved.reshape(moved.shape[:2] + (-1,))


def fine_adjoint(shared_ref, cot_ref, gain_ref, inside_ref, up_ref, conv_ref, back_ref, grad_ref, lifted_ref, norm_ref, rows_ref, taps_ref):
    slab, rows = back_ref.shape[2], rows_ref.shape[1]
    for p in range(2):
        square = jnp.zeros(shared_ref.shape[2:], F32)
        for t in range(NT):
            value = shared_ref[t, p].astype(F32)
            square = square + value * value
        mean = jnp.sum(square, axis=-1, keepdims=True) * (1.0 / C_FINE)
        scale = lax.rsqrt(mean + EPS)
        weighted = jnp.zeros(shared_ref.shape[2:], F32)
        for t in range(NT):
            value = shared_ref[t, p].astype(F32)
            gain = gain_ref[t]
            inner = slope(value * scale * gain) * shared_ref[t, 2 + p].astype(F32) * gain
            weighted = weighted + inner * value
            norm_ref[t] = inner * scale
        total = jnp.sum(weighted, axis=-1, keepdims=True)
        factor = scale * scale * scale * total * (1.0 / C_FINE)
        keep = inside_ref[p] > 0.0
        lifted = jnp.zeros((shared_ref.shape[2], up_ref.shape[2]), F32)
        for t in range(NT):
            value = shared_ref[t, p].astype(F32)
            grad = cot_ref[t, p].astype(F32) + (norm_ref[t] - value * factor)
            grad = jnp.where(keep, grad, 0.0).astype(BF16)
            grad_ref[t, p] = grad
            lifted = lifted + dot_t(grad, up_ref[p, t])
        if p == 0:
            first = lifted
        else:
            lifted = (first + lifted).astype(BF16).astype(F32)
    for s in range(2):
        rows_ref[s] = lifted[s * rows : (s + 1) * rows]
        lifted_ref[s] = rows_ref[s, 2 : 2 + slab, :192].astype(BF16)
        for k in range(5):
            taps_ref[s * slab : (s + 1) * slab, k * 128 : (k + 1) * 128] = rows_ref[
                s, 4 - k : 4 - k + slab, :128
            ].astype(BF16)
        for k in (0, 2, 4):
            tail = rows_ref[s, 4 - k : 4 - k + slab, 128:256]
            if k < 4:
                tail = tail + pltpu.roll(rows_ref[s, 3 - k : 3 - k + slab, 128:256], 64, 1)
            taps_ref[s * slab : (s + 1) * slab, 640 + k * 64 : 768 + k * 64] = tail.astype(BF16)
    for t in range(NT):
        back = dot_t(taps_ref[...], conv_ref[192 * t : 192 * (t + 1), :]).astype(BF16)
        for s in range(2):
            back_ref[t, s] = back[s * slab : (s + 1) * slab]


def slope(value):
    square = value * value
    bend = jnp.tanh(SQRT_2_PI * (value + 0.044715 * (square * value)))
    half = 0.5 * (1.0 + bend)
    return half + 0.5 * value * (1.0 - bend * bend) * (
        SQRT_2_PI * (1.0 + (3 * 0.044715) * square)
    )


def run_fine_adjoint(shared, cot, gain, inside, up_phases, flat, slab):
    whole = pl.BlockSpec(memory_space=pltpu.VMEM)
    rows = shared.shape[2] // 2
    return pl.pallas_call(
        fine_adjoint,
        grid=(1,),
        in_specs=[whole] * 5 + [pl.BlockSpec((C_COARSE, 1024), lambda i: (0, 0))],
        out_specs=[whole] * 3,
        out_shape=[
            jax.ShapeDtypeStruct((NT, 2, slab, 192), BF16),
            jax.ShapeDtypeStruct(cot.shape, BF16),
            jax.ShapeDtypeStruct((2, slab, 192), BF16),
        ],
        scratch_shapes=[
            pltpu.VMEM((NT,) + shared.shape[2:], F32),
            pltpu.VMEM((2, rows, 256), F32),
            pltpu.VMEM((2 * slab, 1024), BF16),
        ],
        compiler_params=pltpu.CompilerParams(vmem_limit_bytes=40 * 2**20),
        name="fine_adjoint",
    )(shared, cot, gain, inside, up_phases, flat)


def fine_back(stacked_ref, weight_ref, back_ref):
    total = jnp.zeros(back_ref.shape, F32)
    for t in range(NT):
        total = total + dot_t(stacked_ref[t], weight_ref[t])
    back_ref[...] = total.astype(BF16)


def run_fine_back(stacked, weight):
    whole = pl.BlockSpec(memory_space=pltpu.VMEM)
    return pl.pallas_call(
        fine_back,
        in_specs=[whole] * 2,
        out_specs=whole,
        out_shape=jax.ShapeDtypeStruct((stacked.shape[1], weight.shape[1]), BF16),
        name="fine_back",
    )(stacked, weight)


def per_device(trunk, w_out, gain_coarse, w_conv1, w_up, skip, gain_fine, w_conv2, cotangent):
    rank = lax.axis_index("tensor")
    place = lax.axis_index("seq")
    part_coarse, part_fine = C_COARSE // NT, C_FINE // NT
    seqs, slab = trunk.shape[0], trunk.shape[1]

    turned = [
        ((8 * a + b) * NT + t, (8 * t + b) * NT + a)
        for a in range(8)
        for b in range(8)
        for t in range(8)
    ]
    up_shard = w_up.reshape(24, 192)
    out_shard = w_out.T
    conv2_flat = jnp.transpose(w_conv2, (1, 0, 2)).reshape(12, 480)
    conv2_shard = jnp.concatenate([conv2_flat[:, :240], conv2_flat[:, 240:]], axis=0)
    both_turned = lax.ppermute(
        jnp.concatenate([out_shard, up_shard, conv2_shard], axis=1), ("seq", "tensor"), turned
    )
    conv1_turned = jnp.transpose(w_conv1, (1, 0, 2))
    conv1_shard = jnp.concatenate(
        [conv1_turned[:, :, :128].reshape(24, 640), conv1_turned[:, :, 128:].reshape(24, 320)],
        axis=1,
    )
    packed = jnp.concatenate(
        [
            both_turned[:, :192],
            conv1_shard,
            jnp.zeros((24, 64), BF16),
            up_shard,
            both_turned[:, 192:384],
            out_shard,
            conv2_shard,
            both_turned[:, 384:],
            jnp.zeros((24, 96), BF16),
        ],
        axis=1,
    )
    paired = lax.all_gather(packed, "seq", axis=0, axis_index_groups=Y_PAIRS)
    gathered = lax.all_gather(
        paired[:, :, 192:], "seq", axis=1, tiled=True, axis_index_groups=Z_CORES
    )
    gathered = with_layout_constraint(gathered, Layout(major_to_minor=(0, 1, 2)))
    flat = gathered.reshape(C_COARSE, -1)
    conv1_w = flat[:, :960]
    up_w = flat[:, 1024:1216]
    up_turned_w = flat[:, 1216:1408].reshape(NT, part_coarse, 192)
    out_t = flat[:, 1408:1600]
    conv2_w = (
        gathered[:, :, 1600:1840]
        .reshape(2, 32, 2, 12, 240)
        .transpose(0, 1, 3, 2, 4)
        .reshape(C_FINE, 480)
    )

    conv2_turned_w = (
        gathered[:, :, 1840:2080]
        .reshape(NT, 8, 2, 12, 240)
        .transpose(0, 1, 3, 2, 4)
        .reshape(NT, part_fine, 480)
    )

    trunk_ext = neighbours(trunk, 4)
    skip_ext = neighbours(skip, 4)
    cot_ext = neighbours(cotangent, 8)
    fine_rows = 2 * slab + 8
    index = place * slab - 2 + lax.broadcasted_iota(jnp.int32, (1, slab + 4, 1), 1)
    inside = (index >= 0) & (index < slab * lax.axis_size("seq"))
    inside_rows = jnp.broadcast_to(inside, (2, 2, slab + 4, 1)).astype(F32)
    skip_phases = jnp.moveaxis(skip_ext.reshape(seqs, slab + 4, 2, part_fine), 2, 0)

    both = share(
        jnp.concatenate([trunk_ext, cot_ext.reshape(seqs, slab + 8, 2 * part_fine)], axis=0)
    )
    trunk_blocks = both[:, :seqs]
    rows = slab + 4
    cot_planes = jnp.moveaxis(
        both[:, seqs:].reshape(NT, seqs, slab + 8, 2, part_fine), 3, 1
    )
    cot_phases = cot_planes[:, :, :, 2 : 2 + rows].reshape(NT, 2, seqs * rows, part_fine)

    def tap(p, k):
        offset = p - k + 2
        q, start = offset % 2, 2 + offset // 2
        return cot_planes[:, q, :, start : start + rows]

    stacked = jnp.stack(
        [jnp.concatenate([tap(p, k) for k in range(5)], axis=-1) for p in range(2)], axis=1
    ).reshape(NT, 2 * seqs * rows, 5 * part_fine)
    out_turned = lax.all_gather(
        paired[:, :, :192], "seq", axis=1, tiled=True, axis_index_groups=Z_CORES
    ).reshape(NT, part_coarse, 192)
    projected = lax.dot_general(
        trunk_blocks, out_turned, (((0, 3), (0, 2)), ((), ())), preferred_element_type=F32
    ).astype(BF16)
    projected_full = lanes(share(projected)).astype(F32)
    scale_coarse = lax.rsqrt(
        jnp.mean(projected_full * projected_full, axis=-1, keepdims=True) + EPS
    )
    act_coarse = jax.nn.gelu(projected_full * scale_coarse * gain_coarse).astype(BF16)

    taps = dot(act_coarse, conv1_w)
    wide = sum(taps[:, k : k + rows, k * 128 : (k + 1) * 128] for k in range(5))
    tail = sum(taps[:, k : k + rows, 640 + k * 64 : 704 + k * 64] for k in range(5))
    mixed = jnp.concatenate([wide, tail], axis=2)
    lifted = (projected[:, 2 : 2 + rows].astype(F32) + mixed).astype(BF16)

    lifted_full = lanes(share(lifted))
    back_piece = run_fine_back(stacked, conv2_turned_w).reshape(2, seqs, rows, part_fine)
    upper = dot(lifted_full, up_w)
    upper = jnp.stack([upper[..., :part_fine], upper[..., part_fine:]])
    merged = jnp.where(inside, upper + skip_phases.astype(F32), 0.0).astype(BF16)
    second = share(
        jnp.concatenate([merged, back_piece], axis=0).reshape(4, seqs * rows, part_fine)
    )

    up_phases = jnp.pad(
        up_turned_w.reshape(NT, part_coarse, 2, part_fine).transpose(2, 0, 1, 3),
        ((0, 0), (0, 0), (0, 64), (0, 0)),
    )
    back_blocks, grad_blocks, lifted_grad = run_fine_adjoint(
        second,
        cot_phases,
        gain_fine.reshape(NT, 1, part_fine),
        inside_rows.reshape(2, seqs * rows, 1),
        up_phases,
        flat,
        slab,
    )
    third = exchange(back_blocks)
    back_coarse = jnp.sum(third.astype(F32), axis=0)

    own = projected[:, 4 : 4 + slab].astype(F32)
    own_gain = lax.dynamic_slice_in_dim(gain_coarse, rank * part_coarse, part_coarse, 0)
    scale = scale_coarse[:, 4 : 4 + slab]
    _, pull_gelu = jax.vjp(jax.nn.gelu, own * scale * own_gain)
    inner = pull_gelu(back_coarse)[0] * own_gain
    share_sum = jnp.sum(inner * own, axis=-1, keepdims=True)
    high = share_sum.astype(BF16)
    low = (share_sum - high.astype(F32)).astype(BF16)
    direct = (lifted_grad.astype(F32) + scale * inner).astype(BF16)
    fourth = share(
        jnp.concatenate([direct, high, low, jnp.zeros((seqs, slab, 62), BF16)], axis=2)
    )
    total = jnp.sum(fourth[..., 192:194].astype(F32), axis=(0, 3))[..., None]
    factor = scale * scale * scale * total * (1.0 / C_COARSE)
    projected_grad = (
        lanes(fourth[..., :192]).astype(F32) - projected_full[:, 4 : 4 + slab] * factor
    ).astype(BF16)
    trunk_grad = dot(projected_grad, out_t).astype(BF16)

    merged_full = (
        second[:, :2]
        .reshape(NT, 2, seqs, rows, part_fine)
        .transpose(2, 3, 1, 0, 4)
        .reshape(seqs, fine_rows, C_FINE)
        .astype(F32)
    )
    scaled = merged_full * lax.rsqrt(
        jnp.mean(merged_full * merged_full, axis=-1, keepdims=True) + EPS
    )
    act_fine = jax.nn.gelu(scaled * gain_fine).astype(BF16)
    fine_taps = dot(act_fine, conv2_w)
    fine_mixed = sum(
        fine_taps[:, 2 + k : 2 + k + 2 * slab, k * part_fine : (k + 1) * part_fine]
        for k in range(5)
    )

    def natural(phases):
        moved = jnp.moveaxis(phases.reshape(2, seqs, rows, part_fine)[:, :, 2 : 2 + slab], 0, 2)
        return moved.reshape(seqs, 2 * slab, part_fine)

    decoded = (natural(merged).astype(F32) + fine_mixed).astype(BF16)
    skip_grad = natural(lax.dynamic_index_in_dim(grad_blocks, rank, 0, keepdims=False))
    return (decoded, skip_grad, trunk_grad)


def solution(mesh):
    in_specs = (
        P(None, "seq", "tensor"),
        P("tensor", "seq"),
        P(),
        P(None, "seq", "tensor"),
        P("seq", None, "tensor"),
        P(None, "seq", "tensor"),
        P(),
        P(None, "seq", "tensor"),
        P(None, "seq", "tensor"),
    )
    out_specs = (P(None, "seq", "tensor"), P(None, "seq", "tensor"), P(None, "seq", "tensor"))

    return jax.shard_map(
        per_device, mesh=mesh, in_specs=in_specs, out_specs=out_specs, check_vma=False
    )
```

```python
import math

import jax
import jax.numpy as jnp
from jax import lax
from jax.experimental import pallas as pl
from jax.experimental.layout import Layout, with_layout_constraint
from jax.experimental.pallas import tpu as pltpu
from jax.sharding import PartitionSpec as P

C_COARSE = 1536
C_FINE = 768
EPS = 1e-06
SQRT_2_PI = math.sqrt(2.0 / math.pi)
BF16 = jnp.bfloat16
F32 = jnp.float32
NT = 8
Y_PAIRS = [[y * 32 + i for y in range(2)] for i in range(32)]
Z_CORES = [[y * 32 + i for i in range(32)] for y in range(2)]


def dot(left, right):
    return lax.dot_general(
        left, right, (((left.ndim - 1,), (0,)), ((), ())), preferred_element_type=F32
    )


def dot_t(left, right):
    return lax.dot_general(
        left,
        right,
        (((left.ndim - 1,), (right.ndim - 1,)), ((), ())),
        preferred_element_type=F32,
    )


def exchange(blocks):
    return lax.all_to_all(blocks, "tensor", 0, 0)


def share(piece):
    return exchange(jnp.broadcast_to(piece[None], (NT,) + piece.shape))


def neighbours(trunk, cotangent, skip):
    size = lax.axis_size("seq")
    up = [(i, i + 1) for i in range(size - 1)]
    down = [(j, i) for i, j in up]

    def edge(coarse, fine):
        both = jnp.concatenate([cotangent[:, fine], skip[:, fine]], axis=2)
        return jnp.concatenate([trunk[:, coarse], both], axis=1)

    before = lax.ppermute(edge(slice(-4, None), slice(-8, None)), "seq", up)
    after = lax.ppermute(edge(slice(0, 4), slice(0, 8)), "seq", down)
    part = cotangent.shape[2]
    return (
        jnp.concatenate([before[:, :4], trunk, after[:, :4]], axis=1),
        jnp.concatenate([before[:, 4:, :part], cotangent, after[:, 4:, :part]], axis=1),
        jnp.concatenate([before[:, 8:, part:], skip, after[:, 4:8, part:]], axis=1),
    )


def lanes(blocks):
    moved = jnp.moveaxis(blocks, 0, 2)
    return moved.reshape(moved.shape[:2] + (-1,))


def fine_adjoint(shared_ref, cot_ref, gain_ref, inside_ref, up_ref, conv_ref, back_ref, grad_ref, lifted_ref, norm_ref, rows_ref, taps_ref, held_ref, fetched):
    slab, rows = back_ref.shape[2], rows_ref.shape[1]
    fetch = pltpu.make_async_copy(conv_ref.at[:, pl.ds(0, 1024)], held_ref, fetched)
    fetch.start()
    for p in range(2):
        square = jnp.zeros(shared_ref.shape[2:], F32)
        for t in range(NT):
            value = shared_ref[t, p].astype(F32)
            square = square + value * value
        mean = jnp.sum(square, axis=-1, keepdims=True) * (1.0 / C_FINE)
        scale = lax.rsqrt(mean + EPS)
        weighted = jnp.zeros(shared_ref.shape[2:], F32)
        for t in range(NT):
            value = shared_ref[t, p].astype(F32)
            gain = gain_ref[t]
            inner = slope(value * scale * gain) * shared_ref[t, 2 + p].astype(F32) * gain
            weighted = weighted + inner * value
            norm_ref[t] = inner * scale
        total = jnp.sum(weighted, axis=-1, keepdims=True)
        factor = scale * scale * scale * total * (1.0 / C_FINE)
        keep = inside_ref[p] > 0.0
        lifted = jnp.zeros((shared_ref.shape[2], up_ref.shape[2]), F32)
        for t in range(NT):
            value = shared_ref[t, p].astype(F32)
            grad = cot_ref[t, p].astype(F32) + (norm_ref[t] - value * factor)
            grad = jnp.where(keep, grad, 0.0).astype(BF16)
            grad_ref[t, p] = grad
            lifted = lifted + dot_t(grad, up_ref[p, t])
        if p == 0:
            first = lifted
        else:
            lifted = (first + lifted).astype(BF16).astype(F32)
    for s in range(2):
        rows_ref[s] = lifted[s * rows : (s + 1) * rows]
        lifted_ref[s] = rows_ref[s, 2 : 2 + slab, :192].astype(BF16)
        for k in range(5):
            taps_ref[s * slab : (s + 1) * slab, k * 128 : (k + 1) * 128] = rows_ref[
                s, 4 - k : 4 - k + slab, :128
            ].astype(BF16)
        for k in (0, 2, 4):
            tail = rows_ref[s, 4 - k : 4 - k + slab, 128:256]
            if k < 4:
                tail = tail + pltpu.roll(rows_ref[s, 3 - k : 3 - k + slab, 128:256], 64, 1)
            taps_ref[s * slab : (s + 1) * slab, 640 + k * 64 : 768 + k * 64] = tail.astype(BF16)
    fetch.wait()
    for t in range(NT):
        back = dot_t(taps_ref[...], held_ref[192 * t : 192 * (t + 1), :]).astype(BF16)
        for s in range(2):
            back_ref[t, s] = back[s * slab : (s + 1) * slab]


def slope(value):
    square = value * value
    bend = jnp.tanh(SQRT_2_PI * (value + 0.044715 * (square * value)))
    half = 0.5 * (1.0 + bend)
    return half + 0.5 * value * (1.0 - bend * bend) * (
        SQRT_2_PI * (1.0 + (3 * 0.044715) * square)
    )


def run_fine_adjoint(shared, cot, gain, inside, up_phases, flat, slab):
    whole = pl.BlockSpec(memory_space=pltpu.VMEM)
    rows = shared.shape[2] // 2
    return pl.pallas_call(
        fine_adjoint,
        in_specs=[whole] * 5 + [pl.BlockSpec(memory_space=pltpu.HBM)],
        out_specs=[whole] * 3,
        out_shape=[
            jax.ShapeDtypeStruct((NT, 2, slab, 192), BF16),
            jax.ShapeDtypeStruct(cot.shape, BF16),
            jax.ShapeDtypeStruct((2, slab, 192), BF16),
        ],
        scratch_shapes=[
            pltpu.VMEM((NT,) + shared.shape[2:], F32),
            pltpu.VMEM((2, rows, 256), F32),
            pltpu.VMEM((2 * slab, 1024), BF16),
            pltpu.VMEM((C_COARSE, 1024), BF16),
            pltpu.SemaphoreType.DMA,
        ],
        compiler_params=pltpu.CompilerParams(vmem_limit_bytes=40 * 2**20),
        name="fine_adjoint",
    )(shared, cot, gain, inside, up_phases, flat)


def fine_back(stacked_ref, weight_ref, back_ref):
    total = jnp.zeros(back_ref.shape, F32)
    for t in range(NT):
        total = total + dot_t(stacked_ref[t], weight_ref[t])
    back_ref[...] = total.astype(BF16)


def run_fine_back(stacked, weight):
    whole = pl.BlockSpec(memory_space=pltpu.VMEM)
    return pl.pallas_call(
        fine_back,
        in_specs=[whole] * 2,
        out_specs=whole,
        out_shape=jax.ShapeDtypeStruct((stacked.shape[1], weight.shape[1]), BF16),
        name="fine_back",
    )(stacked, weight)


def per_device(trunk, w_out, gain_coarse, w_conv1, w_up, skip, gain_fine, w_conv2, cotangent):
    rank = lax.axis_index("tensor")
    place = lax.axis_index("seq")
    part_coarse, part_fine = C_COARSE // NT, C_FINE // NT
    seqs, slab = trunk.shape[0], trunk.shape[1]

    turned = [
        ((8 * a + b) * NT + t, (8 * t + b) * NT + a)
        for a in range(8)
        for b in range(8)
        for t in range(8)
    ]
    up_shard = w_up.reshape(24, 192)
    out_shard = w_out.T
    conv2_flat = jnp.transpose(w_conv2, (1, 0, 2)).reshape(12, 480)
    conv2_shard = jnp.concatenate([conv2_flat[:, :240], conv2_flat[:, 240:]], axis=0)
    both_turned = lax.ppermute(
        jnp.concatenate([out_shard, up_shard, conv2_shard], axis=1), ("seq", "tensor"), turned
    )
    conv1_turned = jnp.transpose(w_conv1, (1, 0, 2))
    conv1_shard = jnp.concatenate(
        [conv1_turned[:, :, :128].reshape(24, 640), conv1_turned[:, :, 128:].reshape(24, 320)],
        axis=1,
    )
    packed = jnp.concatenate(
        [
            both_turned[:, :192],
            conv1_shard,
            jnp.zeros((24, 64), BF16),
            up_shard,
            both_turned[:, 192:384],
            out_shard,
            conv2_shard,
            both_turned[:, 384:],
            jnp.zeros((24, 96), BF16),
        ],
        axis=1,
    )
    paired = lax.all_gather(packed, "seq", axis=0, axis_index_groups=Y_PAIRS)
    gathered = lax.all_gather(
        paired[:, :, 192:], "seq", axis=1, tiled=True, axis_index_groups=Z_CORES
    )
    gathered = with_layout_constraint(gathered, Layout(major_to_minor=(0, 1, 2)))
    flat = gathered.reshape(C_COARSE, -1)
    conv1_w = flat[:, :960]
    up_w = flat[:, 1024:1216]
    up_turned_w = flat[:, 1216:1408].reshape(NT, part_coarse, 192)
    out_t = flat[:, 1408:1600]
    conv2_w = (
        gathered[:, :, 1600:1840]
        .reshape(2, 32, 2, 12, 240)
        .transpose(0, 1, 3, 2, 4)
        .reshape(C_FINE, 480)
    )

    conv2_turned_w = (
        gathered[:, :, 1840:2080]
        .reshape(NT, 8, 2, 12, 240)
        .transpose(0, 1, 3, 2, 4)
        .reshape(NT, part_fine, 480)
    )

    trunk_ext, cot_ext, skip_ext = neighbours(trunk, cotangent, skip)
    fine_rows = 2 * slab + 8
    index = place * slab - 2 + lax.broadcasted_iota(jnp.int32, (1, slab + 4, 1), 1)
    inside = (index >= 0) & (index < slab * lax.axis_size("seq"))
    inside_rows = jnp.broadcast_to(inside, (2, 2, slab + 4, 1)).astype(F32)
    skip_phases = jnp.moveaxis(skip_ext.reshape(seqs, slab + 4, 2, part_fine), 2, 0)

    both = share(
        jnp.concatenate([trunk_ext, cot_ext.reshape(seqs, slab + 8, 2 * part_fine)], axis=0)
    )
    trunk_blocks = both[:, :seqs]
    rows = slab + 4
    cot_planes = jnp.moveaxis(
        both[:, seqs:].reshape(NT, seqs, slab + 8, 2, part_fine), 3, 1
    )
    cot_phases = cot_planes[:, :, :, 2 : 2 + rows].reshape(NT, 2, seqs * rows, part_fine)

    def tap(p, k):
        offset = p - k + 2
        q, start = offset % 2, 2 + offset // 2
        return cot_planes[:, q, :, start : start + rows]

    stacked = jnp.stack(
        [jnp.concatenate([tap(p, k) for k in range(5)], axis=-1) for p in range(2)], axis=1
    ).reshape(NT, 2 * seqs * rows, 5 * part_fine)
    out_turned = lax.all_gather(
        paired[:, :, :192], "seq", axis=1, tiled=True, axis_index_groups=Z_CORES
    ).reshape(NT, part_coarse, 192)
    projected = lax.dot_general(
        trunk_blocks, out_turned, (((0, 3), (0, 2)), ((), ())), preferred_element_type=F32
    ).astype(BF16)
    projected_full = lanes(share(projected)).astype(F32)
    scale_coarse = lax.rsqrt(
        jnp.mean(projected_full * projected_full, axis=-1, keepdims=True) + EPS
    )
    act_coarse = jax.nn.gelu(projected_full * scale_coarse * gain_coarse).astype(BF16)

    taps = dot(act_coarse, conv1_w)
    wide = sum(taps[:, k : k + rows, k * 128 : (k + 1) * 128] for k in range(5))
    tail = sum(taps[:, k : k + rows, 640 + k * 64 : 704 + k * 64] for k in range(5))
    mixed = jnp.concatenate([wide, tail], axis=2)
    lifted = (projected[:, 2 : 2 + rows].astype(F32) + mixed).astype(BF16)

    lifted_full = lanes(share(lifted))
    back_piece = run_fine_back(stacked, conv2_turned_w).reshape(2, seqs, rows, part_fine)
    upper = dot(lifted_full, up_w)
    upper = jnp.stack([upper[..., :part_fine], upper[..., part_fine:]])
    merged = jnp.where(inside, upper + skip_phases.astype(F32), 0.0).astype(BF16)
    second = share(
        jnp.concatenate([merged, back_piece], axis=0).reshape(4, seqs * rows, part_fine)
    )

    up_phases = jnp.pad(
        up_turned_w.reshape(NT, part_coarse, 2, part_fine).transpose(2, 0, 1, 3),
        ((0, 0), (0, 0), (0, 64), (0, 0)),
    )
    back_blocks, grad_blocks, lifted_grad = run_fine_adjoint(
        second,
        cot_phases,
        gain_fine.reshape(NT, 1, part_fine),
        inside_rows.reshape(2, seqs * rows, 1),
        up_phases,
        flat,
        slab,
    )
    third = exchange(back_blocks)
    back_coarse = jnp.sum(third.astype(F32), axis=0)

    own = projected[:, 4 : 4 + slab].astype(F32)
    own_gain = lax.dynamic_slice_in_dim(gain_coarse, rank * part_coarse, part_coarse, 0)
    scale = scale_coarse[:, 4 : 4 + slab]
    _, pull_gelu = jax.vjp(jax.nn.gelu, own * scale * own_gain)
    inner = pull_gelu(back_coarse)[0] * own_gain
    share_sum = jnp.sum(inner * own, axis=-1, keepdims=True)
    high = share_sum.astype(BF16)
    low = (share_sum - high.astype(F32)).astype(BF16)
    direct = (lifted_grad.astype(F32) + scale * inner).astype(BF16)
    fourth = share(
        jnp.concatenate([direct, high, low, jnp.zeros((seqs, slab, 62), BF16)], axis=2)
    )
    total = jnp.sum(fourth[..., 192:194].astype(F32), axis=(0, 3))[..., None]
    factor = scale * scale * scale * total * (1.0 / C_COARSE)
    projected_grad = (
        lanes(fourth[..., :192]).astype(F32) - projected_full[:, 4 : 4 + slab] * factor
    ).astype(BF16)
    trunk_grad = dot(projected_grad, out_t).astype(BF16)

    merged_full = (
        second[:, :2]
        .reshape(NT, 2, seqs, rows, part_fine)
        .transpose(2, 3, 1, 0, 4)
        .reshape(seqs, fine_rows, C_FINE)
        .astype(F32)
    )
    scaled = merged_full * lax.rsqrt(
        jnp.mean(merged_full * merged_full, axis=-1, keepdims=True) + EPS
    )
    act_fine = jax.nn.gelu(scaled * gain_fine).astype(BF16)
    fine_taps = dot(act_fine, conv2_w)
    fine_mixed = sum(
        fine_taps[:, 2 + k : 2 + k + 2 * slab, k * part_fine : (k + 1) * part_fine]
        for k in range(5)
    )

    def natural(phases):
        moved = jnp.moveaxis(phases.reshape(2, seqs, rows, part_fine)[:, :, 2 : 2 + slab], 0, 2)
        return moved.reshape(seqs, 2 * slab, part_fine)

    decoded = (natural(merged).astype(F32) + fine_mixed).astype(BF16)
    skip_grad = natural(lax.dynamic_index_in_dim(grad_blocks, rank, 0, keepdims=False))
    return (decoded, skip_grad, trunk_grad)


def solution(mesh):
    in_specs = (
        P(None, "seq", "tensor"),
        P("tensor", "seq"),
        P(),
        P(None, "seq", "tensor"),
        P("seq", None, "tensor"),
        P(None, "seq", "tensor"),
        P(),
        P(None, "seq", "tensor"),
        P(None, "seq", "tensor"),
    )
    out_specs = (P(None, "seq", "tensor"), P(None, "seq", "tensor"), P(None, "seq", "tensor"))

    return jax.shard_map(
        per_device, mesh=mesh, in_specs=in_specs, out_specs=out_specs, check_vma=False
    )
```

```python
import math

import jax
import jax.numpy as jnp
from jax import lax
from jax.experimental import pallas as pl
from jax.experimental.layout import Layout, with_layout_constraint
from jax.experimental.pallas import tpu as pltpu
from jax.sharding import PartitionSpec as P

C_COARSE = 1536
C_FINE = 768
EPS = 1e-06
SQRT_2_PI = math.sqrt(2.0 / math.pi)
BF16 = jnp.bfloat16
F32 = jnp.float32
NT = 8
Y_PAIRS = [[y * 32 + i for y in range(2)] for i in range(32)]
Z_CORES = [[y * 32 + i for i in range(32)] for y in range(2)]


def dot(left, right):
    return lax.dot_general(
        left, right, (((left.ndim - 1,), (0,)), ((), ())), preferred_element_type=F32
    )


def dot_t(left, right):
    return lax.dot_general(
        left,
        right,
        (((left.ndim - 1,), (right.ndim - 1,)), ((), ())),
        preferred_element_type=F32,
    )


def exchange(blocks):
    return lax.all_to_all(blocks, "tensor", 0, 0)


def share(piece):
    return exchange(jnp.broadcast_to(piece[None], (NT,) + piece.shape))


def neighbours(trunk, cotangent, skip):
    size = lax.axis_size("seq")
    up = [(i, i + 1) for i in range(size - 1)]
    down = [(j, i) for i, j in up]

    def edge(coarse, fine):
        both = jnp.concatenate([cotangent[:, fine], skip[:, fine]], axis=2)
        return jnp.concatenate([trunk[:, coarse], both], axis=1)

    before = lax.ppermute(edge(slice(-4, None), slice(-8, None)), "seq", up)
    after = lax.ppermute(edge(slice(0, 4), slice(0, 8)), "seq", down)
    part = cotangent.shape[2]
    return (
        jnp.concatenate([before[:, :4], trunk, after[:, :4]], axis=1),
        jnp.concatenate([before[:, 4:, :part], cotangent, after[:, 4:, :part]], axis=1),
        jnp.concatenate([before[:, 8:, part:], skip, after[:, 4:8, part:]], axis=1),
    )


def lanes(blocks):
    moved = jnp.moveaxis(blocks, 0, 2)
    return moved.reshape(moved.shape[:2] + (-1,))


def fine_adjoint(shared_ref, cot_ref, gain_ref, inside_ref, up_ref, conv_ref, back_ref, grad_ref, lifted_ref, norm_ref, rows_ref, taps_ref):
    slab, rows = back_ref.shape[2], rows_ref.shape[1]
    for p in range(2):
        square = jnp.zeros(shared_ref.shape[2:], F32)
        for t in range(NT):
            value = shared_ref[t, p].astype(F32)
            square = square + value * value
        mean = jnp.sum(square, axis=-1, keepdims=True) * (1.0 / C_FINE)
        scale = lax.rsqrt(mean + EPS)
        weighted = jnp.zeros(shared_ref.shape[2:], F32)
        for t in range(NT):
            value = shared_ref[t, p].astype(F32)
            gain = gain_ref[t]
            inner = slope(value * scale * gain) * shared_ref[t, 2 + p].astype(F32) * gain
            weighted = weighted + inner * value
            norm_ref[t] = inner * scale
        total = jnp.sum(weighted, axis=-1, keepdims=True)
        factor = scale * scale * scale * total * (1.0 / C_FINE)
        keep = inside_ref[p] > 0.0
        lifted = jnp.zeros((shared_ref.shape[2], up_ref.shape[2]), F32)
        for t in range(NT):
            value = shared_ref[t, p].astype(F32)
            grad = cot_ref[t, p].astype(F32) + (norm_ref[t] - value * factor)
            grad = jnp.where(keep, grad, 0.0).astype(BF16)
            grad_ref[t, p] = grad
            lifted = lifted + dot_t(grad, up_ref[p, t])
        if p == 0:
            first = lifted
        else:
            lifted = (first + lifted).astype(BF16).astype(F32)
    for s in range(2):
        rows_ref[s] = lifted[s * rows : (s + 1) * rows]
        lifted_ref[s] = rows_ref[s, 2 : 2 + slab, :192].astype(BF16)
        for k in range(5):
            taps_ref[s * slab : (s + 1) * slab, k * 128 : (k + 1) * 128] = rows_ref[
                s, 4 - k : 4 - k + slab, :128
            ].astype(BF16)
        for k in (0, 2, 4):
            tail = rows_ref[s, 4 - k : 4 - k + slab, 128:256]
            if k < 4:
                tail = tail + pltpu.roll(rows_ref[s, 3 - k : 3 - k + slab, 128:256], 64, 1)
            taps_ref[s * slab : (s + 1) * slab, 640 + k * 64 : 768 + k * 64] = tail.astype(BF16)
    for t in range(NT):
        back = dot_t(taps_ref[...], conv_ref[192 * t : 192 * (t + 1), :]).astype(BF16)
        for s in range(2):
            back_ref[t, s] = back[s * slab : (s + 1) * slab]


def slope(value):
    square = value * value
    bend = jnp.tanh(SQRT_2_PI * (value + 0.044715 * (square * value)))
    half = 0.5 * (1.0 + bend)
    return half + 0.5 * value * (1.0 - bend * bend) * (
        SQRT_2_PI * (1.0 + (3 * 0.044715) * square)
    )


def run_fine_adjoint(shared, cot, gain, inside, up_phases, flat, slab):
    whole = pl.BlockSpec(memory_space=pltpu.VMEM)
    rows = shared.shape[2] // 2
    return pl.pallas_call(
        fine_adjoint,
        in_specs=[whole] * 6,
        out_specs=[whole] * 3,
        out_shape=[
            jax.ShapeDtypeStruct((NT, 2, slab, 192), BF16),
            jax.ShapeDtypeStruct(cot.shape, BF16),
            jax.ShapeDtypeStruct((2, slab, 192), BF16),
        ],
        scratch_shapes=[
            pltpu.VMEM((NT,) + shared.shape[2:], F32),
            pltpu.VMEM((2, rows, 256), F32),
            pltpu.VMEM((2 * slab, 1024), BF16),
        ],
        compiler_params=pltpu.CompilerParams(vmem_limit_bytes=18 * 2**20),
        name="fine_adjoint",
    )(shared, cot, gain, inside, up_phases, flat)


def fine_back(stacked_ref, weight_ref, back_ref):
    total = jnp.zeros(back_ref.shape, F32)
    for t in range(NT):
        total = total + dot_t(stacked_ref[t], weight_ref[t])
    back_ref[...] = total.astype(BF16)


def run_fine_back(stacked, weight):
    whole = pl.BlockSpec(memory_space=pltpu.VMEM)
    return pl.pallas_call(
        fine_back,
        in_specs=[whole] * 2,
        out_specs=whole,
        out_shape=jax.ShapeDtypeStruct((stacked.shape[1], weight.shape[1]), BF16),
        name="fine_back",
    )(stacked, weight)


def per_device(trunk, w_out, gain_coarse, w_conv1, w_up, skip, gain_fine, w_conv2, cotangent):
    rank = lax.axis_index("tensor")
    place = lax.axis_index("seq")
    part_coarse, part_fine = C_COARSE // NT, C_FINE // NT
    seqs, slab = trunk.shape[0], trunk.shape[1]

    turned = [
        ((8 * a + b) * NT + t, (8 * t + b) * NT + a)
        for a in range(8)
        for b in range(8)
        for t in range(8)
    ]
    up_shard = w_up.reshape(24, 192)
    out_shard = w_out.T
    conv2_flat = jnp.transpose(w_conv2, (1, 0, 2)).reshape(12, 480)
    conv2_shard = jnp.concatenate([conv2_flat[:, :240], conv2_flat[:, 240:]], axis=0)
    both_turned = lax.ppermute(
        jnp.concatenate([out_shard, up_shard, conv2_shard], axis=1), ("seq", "tensor"), turned
    )
    conv1_turned = jnp.transpose(w_conv1, (1, 0, 2))
    conv1_shard = jnp.concatenate(
        [conv1_turned[:, :, :128].reshape(24, 640), conv1_turned[:, :, 128:].reshape(24, 320)],
        axis=1,
    )
    packed = jnp.concatenate(
        [
            conv1_shard,
            jnp.zeros((24, 64), BF16),
            up_shard,
            both_turned[:, 192:384],
            out_shard,
            conv2_shard,
            both_turned[:, 384:],
            both_turned[:, :192],
            jnp.zeros((24, 32), BF16),
        ],
        axis=1,
    )
    paired = lax.all_gather(packed, "seq", axis=0, axis_index_groups=Y_PAIRS)
    gathered = lax.all_gather(
        paired, "seq", axis=1, tiled=True, axis_index_groups=Z_CORES
    )
    gathered = with_layout_constraint(gathered, Layout(major_to_minor=(0, 1, 2)))
    flat = gathered.reshape(C_COARSE, -1)
    conv1_w = flat[:, :960]
    up_w = flat[:, 1024:1216]
    up_turned_w = flat[:, 1216:1408].reshape(NT, part_coarse, 192)
    out_t = flat[:, 1408:1600]
    conv2_w = (
        gathered[:, :, 1600:1840]
        .reshape(2, 32, 2, 12, 240)
        .transpose(0, 1, 3, 2, 4)
        .reshape(C_FINE, 480)
    )

    conv2_turned_w = (
        gathered[:, :, 1840:2080]
        .reshape(NT, 8, 2, 12, 240)
        .transpose(0, 1, 3, 2, 4)
        .reshape(NT, part_fine, 480)
    )

    trunk_ext, cot_ext, skip_ext = neighbours(trunk, cotangent, skip)
    fine_rows = 2 * slab + 8
    index = place * slab - 2 + lax.broadcasted_iota(jnp.int32, (1, slab + 4, 1), 1)
    inside = (index >= 0) & (index < slab * lax.axis_size("seq"))
    inside_rows = jnp.broadcast_to(inside, (2, 2, slab + 4, 1)).astype(F32)
    skip_phases = jnp.moveaxis(skip_ext.reshape(seqs, slab + 4, 2, part_fine), 2, 0)

    both = share(
        jnp.concatenate([trunk_ext, cot_ext.reshape(seqs, slab + 8, 2 * part_fine)], axis=0)
    )
    trunk_blocks = both[:, :seqs]
    rows = slab + 4
    cot_planes = jnp.moveaxis(
        both[:, seqs:].reshape(NT, seqs, slab + 8, 2, part_fine), 3, 1
    )
    cot_phases = cot_planes[:, :, :, 2 : 2 + rows].reshape(NT, 2, seqs * rows, part_fine)

    def tap(p, k):
        offset = p - k + 2
        q, start = offset % 2, 2 + offset // 2
        return cot_planes[:, q, :, start : start + rows]

    stacked = jnp.stack(
        [jnp.concatenate([tap(p, k) for k in range(5)], axis=-1) for p in range(2)], axis=1
    ).reshape(NT, 2 * seqs * rows, 5 * part_fine)
    out_turned = lax.all_gather(
        paired[:, :, 2080:2272], "seq", axis=1, tiled=True, axis_index_groups=Z_CORES
    ).reshape(NT, part_coarse, 192)
    projected = lax.dot_general(
        trunk_blocks, out_turned, (((0, 3), (0, 2)), ((), ())), preferred_element_type=F32
    ).astype(BF16)
    projected_full = lanes(share(projected)).astype(F32)
    scale_coarse = lax.rsqrt(
        jnp.mean(projected_full * projected_full, axis=-1, keepdims=True) + EPS
    )
    act_coarse = jax.nn.gelu(projected_full * scale_coarse * gain_coarse).astype(BF16)

    taps = dot(act_coarse, conv1_w)
    wide = sum(taps[:, k : k + rows, k * 128 : (k + 1) * 128] for k in range(5))
    tail = sum(taps[:, k : k + rows, 640 + k * 64 : 704 + k * 64] for k in range(5))
    mixed = jnp.concatenate([wide, tail], axis=2)
    lifted = (projected[:, 2 : 2 + rows].astype(F32) + mixed).astype(BF16)

    lifted_full = lanes(share(lifted))
    back_piece = run_fine_back(stacked, conv2_turned_w).reshape(2, seqs, rows, part_fine)
    upper = dot(lifted_full, up_w)
    upper = jnp.stack([upper[..., :part_fine], upper[..., part_fine:]])
    merged = jnp.where(inside, upper + skip_phases.astype(F32), 0.0).astype(BF16)
    second = share(
        jnp.concatenate([merged, back_piece], axis=0).reshape(4, seqs * rows, part_fine)
    )

    up_phases = jnp.pad(
        up_turned_w.reshape(NT, part_coarse, 2, part_fine).transpose(2, 0, 1, 3),
        ((0, 0), (0, 0), (0, 64), (0, 0)),
    )
    back_blocks, grad_blocks, lifted_grad = run_fine_adjoint(
        second,
        cot_phases,
        gain_fine.reshape(NT, 1, part_fine),
        inside_rows.reshape(2, seqs * rows, 1),
        up_phases,
        flat[:, :1024],
        slab,
    )
    late, back_blocks = lax.optimization_barrier((second[:, :2], back_blocks))
    third = exchange(back_blocks)
    back_coarse = jnp.sum(third.astype(F32), axis=0)

    own = projected[:, 4 : 4 + slab].astype(F32)
    own_gain = lax.dynamic_slice_in_dim(gain_coarse, rank * part_coarse, part_coarse, 0)
    scale = scale_coarse[:, 4 : 4 + slab]
    _, pull_gelu = jax.vjp(jax.nn.gelu, own * scale * own_gain)
    inner = pull_gelu(back_coarse)[0] * own_gain
    share_sum = jnp.sum(inner * own, axis=-1, keepdims=True)
    high = share_sum.astype(BF16)
    low = (share_sum - high.astype(F32)).astype(BF16)
    direct = (lifted_grad.astype(F32) + scale * inner).astype(BF16)
    fourth = share(
        jnp.concatenate([direct, high, low, jnp.zeros((seqs, slab, 62), BF16)], axis=2)
    )
    total = jnp.sum(fourth[..., 192:194].astype(F32), axis=(0, 3))[..., None]
    factor = scale * scale * scale * total * (1.0 / C_COARSE)
    projected_grad = (
        lanes(fourth[..., :192]).astype(F32) - projected_full[:, 4 : 4 + slab] * factor
    ).astype(BF16)
    trunk_grad = dot(projected_grad, out_t).astype(BF16)

    merged_full = (
        late.reshape(NT, 2, seqs, rows, part_fine)
        .transpose(2, 3, 1, 0, 4)
        .reshape(seqs, fine_rows, C_FINE)
        .astype(F32)
    )
    scaled = merged_full * lax.rsqrt(
        jnp.mean(merged_full * merged_full, axis=-1, keepdims=True) + EPS
    )
    act_fine = jax.nn.gelu(scaled * gain_fine).astype(BF16)
    fine_taps = dot(act_fine, conv2_w)
    fine_mixed = sum(
        fine_taps[:, 2 + k : 2 + k + 2 * slab, k * part_fine : (k + 1) * part_fine]
        for k in range(5)
    )

    def natural(phases):
        moved = jnp.moveaxis(phases.reshape(2, seqs, rows, part_fine)[:, :, 2 : 2 + slab], 0, 2)
        return moved.reshape(seqs, 2 * slab, part_fine)

    decoded = (natural(merged).astype(F32) + fine_mixed).astype(BF16)
    skip_grad = natural(lax.dynamic_index_in_dim(grad_blocks, rank, 0, keepdims=False))
    return (decoded, skip_grad, trunk_grad)


def solution(mesh):
    in_specs = (
        P(None, "seq", "tensor"),
        P("tensor", "seq"),
        P(),
        P(None, "seq", "tensor"),
        P("seq", None, "tensor"),
        P(None, "seq", "tensor"),
        P(),
        P(None, "seq", "tensor"),
        P(None, "seq", "tensor"),
    )
    out_specs = (P(None, "seq", "tensor"), P(None, "seq", "tensor"), P(None, "seq", "tensor"))

    return jax.shard_map(
        per_device, mesh=mesh, in_specs=in_specs, out_specs=out_specs, check_vma=False
    )
```
